256 devices in a mesh: replica: 64 (over x, z, core), shard: 4 (over y).
Axes of the slice: x: 4, y: 4, z: 8, core: 2. Of those that a mesh axis runs over, the one named last changes fastest.
Arguments:
- activations: bfloat16 [65536, 1536], P('replica'), may hold values from -6 to 6
- output_grads: bfloat16 [65536, 4, 1536], P('replica', None, 'shard'), may hold values from -0.00390625 to 0.00390625
- owner: int32 [4], replicated, may hold values from 0 to 3, each once
- step_count: int32 [1], replicated, may hold values from 1 to 40
- statistics: float32 [6144, 2, 1536], P(('replica', 'shard')), may hold values from -6 to 6
- inverse_roots: bfloat16 [6144, 2, 1536], P(('replica', 'shard')), may hold values from -1 to 2, as said below
- first_moment: float32 [6144, 1536], P(('replica', 'shard')), may hold values from -0.6 to 0.6
- second_moment: float32 [6144, 1536], P(('replica', 'shard')), may hold values from 0.005 to 0.05
Outputs:
- new_statistics: float32 [6144, 2, 1536], P(('replica', 'shard'))
- new_first: float32 [6144, 1536], P(('replica', 'shard'))
- new_second: float32 [6144, 1536], P(('replica', 'shard'))
- update: bfloat16 [4, 1536, 1536], P(None, None, 'shard')
The draws below stay inside these ranges and needn't reach their ends.
Inputs may be any that keep to these rules, and one draw needn't show every extreme that they name: A permutation: block b belongs to the group of replicas b' * (16) to (b' + 1) * 16 - 1 with b' = owner[b]. `inverse_roots`: each matrix has positive diagonal entries.
All inputs are finite; a program needn't handle non-finite values.
Results may differ from the reference program's by a relative error of at most 0.0049.
Values may be sent and summed in bfloat16 or wider, within the bound.
No kernel may reach another device: no remote copies, remote signals or barrier semaphores. Data moves between devices by JAX's collectives and lax.ppermute only.
A program may use at most 128 MiB of HBM per device.

```python
import math
import jax
import jax.numpy as jnp
from jax import lax

D = 1536
BLOCKS = 4
TOKENS = 65536


def draw_inverse_roots(key, part):
    base_key = jax.random.fold_in(key, 11)
    key_noise, key_diagonal = jax.random.split(base_key, 2)
    scatter_noise = jax.random.normal(key_noise, (BLOCKS * D, 2, D), jnp.float32) * (0.5 / math.sqrt(D))
    diagonal = jax.random.uniform(key_diagonal, (BLOCKS * D, 2, 1), jnp.float32, 0.5, 1.5)
    within_rows = (jnp.arange(BLOCKS * D, dtype=jnp.int32) % D)[:, None, None]
    column_ids = jnp.arange(D, dtype=jnp.int32)[None, None, :]
    return (scatter_noise + jnp.where(within_rows == column_ids, diagonal, 0.0)).astype(jnp.bfloat16)


def steps_of(stream_key, extent, cuts, low, largest):
    def one(position, shards_of):
        heights = jax.random.uniform(jax.random.fold_in(jax.random.fold_in(stream_key, 6), position), (shards_of,), jnp.float32, low / len(cuts), largest / len(cuts))
        return jnp.repeat(jnp.exp(heights), extent[position] // shards_of).reshape((-1,) + (1,) * (len(extent) - position - 1))

    loudness = one(*cuts[0])
    for cut in cuts[1:]:
        loudness = loudness * one(*cut)
    return loudness


def centred(own_key, dims, deviation, limit, shards=(), kind=jnp.bfloat16):
    values = jax.random.normal(own_key, dims, jnp.float32) * deviation
    if len(shards) > 0:
        values = steps_of(own_key, dims, shards, -0.22, 0.18) * values
    return jnp.clip(values, min=-limit, max=limit).astype(kind)


def setup_inputs(seed: int = 0) -> dict:
    splits = jax.random.split(jax.random.key(seed), 9)
    return {
        "activations": centred(splits[0], (TOKENS, D), 1.0, 6.0, ((0, 64),)),
        "output_grads": centred(splits[1], (TOKENS, BLOCKS, D), (TOKENS * 40) ** -0.5, 0.00390625, ((0, 64), (2, 4))),
        "owner": jax.random.permutation(splits[2], BLOCKS).astype(jnp.int32),
        "step_count": jax.random.randint(splits[3], (1,), 1, 41).astype(jnp.int32),
        "statistics": centred(splits[4], (BLOCKS * D, 2, D), 1.0, 6.0, ((0, 256),), jnp.float32),
        "inverse_roots": draw_inverse_roots(jax.random.fold_in(splits[8], 71), 0),
        "first_moment": centred(splits[6], (BLOCKS * D, D), 0.1, 0.6, ((0, 256),), jnp.float32),
        "second_moment": jnp.clip(jnp.exp(math.log(0.05) - 2.3025851 * jax.random.uniform(splits[7], (BLOCKS * D, D), jnp.float32) ** steps_of(splits[7], (BLOCKS * D, D), ((0, 256),), -0.2, 0.2)), 0.005, 0.05),
    }


beta_stat = 0.9
beta_first = 0.9
beta_second = 0.999
eps_adam = 1e-08
eps_norm = 1e-06

def reference(activations, output_grads, owner, step_count, statistics, inverse_roots, first_moment, second_moment):
    blocks_count = output_grads.shape[1]
    model_width = activations.shape[1]
    slot_ids = jnp.arange(blocks_count, dtype=jnp.int32)
    onehot = (owner[None, :] == slot_ids[:, None]).astype(jnp.int32)
    source = lax.optimization_barrier(jnp.sum(onehot * slot_ids[None, :], axis=1)).astype(jnp.int32)

    def block_grad(block_index):
        douts = lax.dynamic_index_in_dim(output_grads, block_index, 1, keepdims=False)
        return lax.dot_general(activations, douts, (((0,), (0,)), ((), ())), preferred_element_type=jnp.float32)
    exact = lax.map(block_grad, source)
    rounded = exact.astype(jnp.bfloat16)
    stats_slot = statistics.reshape(blocks_count, model_width, 2, model_width)
    roots_slot = inverse_roots.reshape(blocks_count, model_width, 2, model_width)

    def precondition(operands):
        grad_block, stat_block, root_block = operands
        left_gram = lax.dot_general(grad_block, grad_block, (((1,), (1,)), ((), ())), preferred_element_type=jnp.float32)
        right_gram = lax.dot_general(grad_block, grad_block, (((0,), (0,)), ((), ())), preferred_element_type=jnp.float32)
        new_left = beta_stat * stat_block[:, 0, :] + (1.0 - beta_stat) * left_gram
        new_right = beta_stat * stat_block[:, 1, :] + (1.0 - beta_stat) * right_gram
        right_part = lax.dot_general(grad_block, root_block[:, 1, :], (((1,), (1,)), ((), ())), preferred_element_type=jnp.float32)
        precond = jnp.dot(root_block[:, 0, :].astype(jnp.float32), right_part, precision=lax.Precision.HIGHEST)
        return (jnp.stack([new_left, new_right], axis=1), precond)
    new_stats, precond = lax.map(precondition, (rounded, stats_slot, roots_slot))
    flat_grad = exact.reshape(blocks_count * model_width, model_width)
    count_float = step_count[0].astype(jnp.float32)
    first_new = beta_first * first_moment + (1.0 - beta_first) * flat_grad
    second_new = beta_second * second_moment + (1.0 - beta_second) * flat_grad * flat_grad
    first_hat = first_new / (1.0 - jnp.power(beta_first, count_float))
    second_hat = second_new / (1.0 - jnp.power(beta_second, count_float))
    adam_dir = first_hat / (jnp.sqrt(second_hat) + eps_adam)
    adam_squares = lax.optimization_barrier(jnp.sum((adam_dir * adam_dir).reshape(blocks_count, -1), axis=1))
    precond_squares = lax.optimization_barrier(jnp.sum((precond * precond).reshape(blocks_count, -1), axis=1))
    scale = jnp.sqrt(adam_squares) / (jnp.sqrt(precond_squares) + eps_norm)
    grafted = (precond * scale[:, None, None]).astype(jnp.bfloat16)
    update = jnp.take(grafted, owner, axis=0)
    return (new_stats.reshape(blocks_count * model_width, 2, model_width), first_new, second_new, update)
```

```python
import jax
import jax.numpy as jnp
from jax import lax
from jax.experimental import pallas as pl
from jax.experimental.pallas import tpu as pltpu
from jax.sharding import Mesh
from jax.sharding import PartitionSpec as P

SIZES = {"x": 4, "z": 8, "c": 2, "y": 4}
REPLICA = ("x", "z", "c")
EVERY = ("x", "z", "c", "y")
PLANE = ("z", "c", "y")

beta_stat = 0.9
beta_first = 0.9
beta_second = 0.999
eps_adam = 1e-08
eps_norm = 1e-06


def shifted(value, axis, by):
    n = SIZES[axis]
    return lax.ppermute(value, axis, [(i, (i + by) % n) for i in range(n)])


def outward(n):
    return sorted(range(1, n), key=lambda d: -min(d, n - d))


def window(pieces, start, count, axis):
    return lax.dynamic_slice_in_dim(jnp.concatenate(pieces, axis), start, count, axis)


def gathered(value, axis, dim):
    n = SIZES[axis]
    length = value.shape[dim]
    came = {0: value}
    for d in outward(n):
        came[d] = shifted(value, axis, d)
    ring = [came[(-k) % n] for k in range(n)]
    start = (-lax.axis_index(axis)) % n
    return window(ring + ring[:-1], start * length, n * length, dim)


def scattered_sum(pieces, axis):
    n = SIZES[axis]
    turned = lax.dynamic_slice_in_dim(
        jnp.concatenate([pieces, pieces[:-1]], 0), lax.axis_index(axis), n, 0
    )
    total = turned[0]
    for d in outward(n):
        total = total + shifted(turned[d].astype(jnp.bfloat16), axis, d).astype(jnp.float32)
    return total


def by_core(mine, theirs, core, dim):
    return jnp.where(
        core == 0, jnp.stack([mine, theirs], dim), jnp.stack([theirs, mine], dim)
    )


def place_kernel(distance, core, *refs):
    out = refs[-1]
    mine, theirs = (refs[:4], refs[4:8])
    block = pl.program_id(0)
    for d in range(4):
        for k in range(2):

            @pl.when((distance[block] == d) & (core[0] == k))
            def _():
                out[0, :, k] = mine[d][...]
                out[0, :, 1 - k] = theirs[d][...]


def place_blocks(distance, core, mine, theirs):
    rows, width = mine[0].shape
    part = (8, rows // 8, width)
    whole = pl.BlockSpec(part, lambda b, *_: (0, 0, 0))
    out = pl.pallas_call(
        place_kernel,
        grid_spec=pltpu.PrefetchScalarGridSpec(
            num_scalar_prefetch=2,
            grid=(4,),
            in_specs=[whole] * 8,
            out_specs=pl.BlockSpec((1, 8, 2, *part[1:]), lambda b, *_: (b, 0, 0, 0, 0)),
        ),
        out_shape=jax.ShapeDtypeStruct((4, 8, 2, *part[1:]), jnp.bfloat16),
        compiler_params=pltpu.CompilerParams(vmem_limit_bytes=32 << 20),
        cost_estimate=pl.CostEstimate(flops=0, bytes_accessed=16 * rows * width, transcendentals=0),
        name="place_blocks",
    )(distance, core, *[v.reshape(part) for v in mine + theirs])
    return out.reshape(4, 2 * rows, width)


def root_pairs():
    pairs = []
    for z in range(8):
        for c in range(2):
            for y in range(4):
                line = (z % 2) * 8 + c * 4 + y
                pairs.append(((z * 2 + c) * 4 + y, line * 4 + z // 2))
    return pairs


def body(
    activations,
    output_grads,
    owner,
    step_count,
    statistics,
    inverse_roots,
    first_moment,
    second_moment,
):
    bf, f32 = (jnp.bfloat16, jnp.float32)
    width = activations.shape[1]
    blocks, cols = output_grads.shape[1:]
    span = statistics.shape[0]
    slab = 4 * span
    x, z, core, y = (lax.axis_index(a) for a in EVERY)
    slots = jnp.arange(blocks, dtype=jnp.int32)
    source = jnp.sum((owner[None, :] == slots[:, None]).astype(jnp.int32) * slots[None, :], axis=1)

    right_rows = lax.ppermute(inverse_roots[:, 1, :], PLANE, root_pairs())
    right_root = lax.all_gather(right_rows, ("z", "c"), axis=0, tiled=True)
    left_root = lax.all_gather(inverse_roots[:, 0, :], ("z", "y"), axis=0, tiled=True)

    product = lax.dot_general(
        activations,
        output_grads.reshape(activations.shape[0], blocks * cols),
        (((0,), (0,)), ((), ())),
        preferred_element_type=f32,
    ).reshape(8, 2, slab, blocks * cols)
    total = None
    for d in (2, 1, 3, 0):
        first = lax.dynamic_index_in_dim(source, (x + d) % 4, 0, keepdims=False) * cols

        def half(which):
            return lax.dynamic_slice(product, (0, which, 0, first), (8, 1, slab, cols))[:, 0]

        pair = half(core) + shifted(half(1 - core).astype(bf), "c", 1).astype(f32)
        if d:
            pair = shifted(pair.astype(bf), "x", d).astype(f32)
        total = pair if total is None else total + pair
    reduced = scattered_sum(total, "z")
    slab_rows = gathered(reduced.astype(bf), "y", 1)

    right_part = lax.dot_general(
        slab_rows, right_root, (((1,), (1,)), ((), ())), preferred_element_type=f32
    ).astype(bf)
    right_half = gathered(right_part, "z", 0).reshape(8, slab, cols)
    right_all = by_core(right_half, shifted(right_half, "c", 1), core, 1).reshape(width, cols)
    precond = jnp.dot(left_root, right_all, preferred_element_type=f32)

    rounded = lax.dynamic_slice_in_dim(slab_rows, y * span, span, 0)
    exact = rounded.astype(f32)
    count = step_count[0].astype(f32)
    first_new = beta_first * first_moment + (1.0 - beta_first) * exact
    second_new = beta_second * second_moment + (1.0 - beta_second) * exact * exact
    first_hat = first_new / (1.0 - jnp.power(beta_first, count))
    second_hat = second_new / (1.0 - jnp.power(beta_second, count))
    adam = first_hat / (jnp.sqrt(second_hat) + eps_adam)
    adam_squares = lax.psum(jnp.sum(adam * adam), "z")
    squares = lax.psum(jnp.stack([adam_squares, jnp.sum(precond * precond)]), ("c", "y"))
    scale = jnp.sqrt(squares[0]) / (jnp.sqrt(squares[1]) + eps_norm)
    grafted = (precond * scale).astype(bf)
    mine, theirs = ([grafted] * 4, [shifted(grafted, "c", 1)] * 4)
    for d in (2, 1, 3):
        mine[d] = shifted(grafted, "x", d)
        theirs[d] = shifted(mine[d], "c", 1)
    update = place_blocks((x - owner) % 4, core.reshape(1), mine, theirs)

    half_grad = lax.all_gather(slab_rows, "z", axis=0)
    full_grad = by_core(half_grad, shifted(half_grad, "c", 1), core, 1).reshape(width, width)
    first_column = ((z * 2 + core) * 4 + y) * span
    grad_columns = lax.dynamic_slice_in_dim(full_grad, first_column, span, 1)
    left_gram = lax.dot_general(
        rounded, full_grad, (((1,), (1,)), ((), ())), preferred_element_type=f32
    )
    right_gram = lax.dot_general(
        grad_columns, full_grad, (((0,), (0,)), ((), ())), preferred_element_type=f32
    )
    new_stats = beta_stat * statistics + (1.0 - beta_stat) * jnp.stack([left_gram, right_gram], 1)
    return (new_stats, first_new, second_new, update)


def solution(mesh):
    torus = Mesh(mesh.devices.reshape(*SIZES.values()), EVERY)
    placed = (
        P(REPLICA, None),
        P(REPLICA, None, "y"),
        P(),
        P(),
        P(EVERY, None, None),
        P(EVERY, None, None),
        P(EVERY, None),
        P(EVERY, None),
    )
    return jax.shard_map(
        body,
        mesh=torus,
        in_specs=placed,
        out_specs=(P(EVERY, None, None), P(EVERY, None), P(EVERY, None), P(None, None, "y")),
        check_vma=False,
    )
```

```python
import jax
import jax.numpy as jnp
from jax import lax
from jax.experimental import pallas as pl
from jax.experimental.pallas import tpu as pltpu
from jax.sharding import Mesh
from jax.sharding import PartitionSpec as P

SIZES = {"x": 4, "z": 8, "c": 2, "y": 4}
REPLICA = ("x", "z", "c")
EVERY = ("x", "z", "c", "y")
PLANE = ("z", "c", "y")

beta_stat = 0.9
beta_first = 0.9
beta_second = 0.999
eps_adam = 1e-08
eps_norm = 1e-06


def shifted(value, axis, by):
    n = SIZES[axis]
    return lax.ppermute(value, axis, [(i, (i + by) % n) for i in range(n)])


def outward(n):
    return sorted(range(1, n), key=lambda d: -min(d, n - d))


def window(pieces, start, count, axis):
    return lax.dynamic_slice_in_dim(jnp.concatenate(pieces, axis), start, count, axis)


def gathered(value, axis, dim):
    n = SIZES[axis]
    length = value.shape[dim]
    came = {0: value}
    for d in outward(n):
        came[d] = shifted(value, axis, d)
    ring = [came[(-k) % n] for k in range(n)]
    start = (-lax.axis_index(axis)) % n
    return window(ring + ring[:-1], start * length, n * length, dim)


def both_ways(value, apart):
    pairs = [(2 * i, 2 * ((i + apart) % 8)) for i in range(8)]
    if apart != 4:
        pairs += [(2 * i + 1, 2 * ((i - apart) % 8) + 1) for i in range(8)]
    return lax.ppermute(value, ("z", "c"), pairs)


def by_core(mine, theirs, core, dim):
    return jnp.where(
        core == 0, jnp.stack([mine, theirs], dim), jnp.stack([theirs, mine], dim)
    )


def place_kernel(distance, core, *refs):
    out = refs[-1]
    mine, theirs = (refs[:4], refs[4:8])
    block = pl.program_id(0)
    for d in range(4):
        for k in range(2):

            @pl.when((distance[block] == d) & (core[0] == k))
            def _():
                out[0, :, k] = mine[d][...]
                out[0, :, 1 - k] = theirs[d][...]


def place_blocks(distance, core, mine, theirs):
    rows, width = mine[0].shape
    part = (8, rows // 8, width)
    whole = pl.BlockSpec(part, lambda b, *_: (0, 0, 0))
    out = pl.pallas_call(
        place_kernel,
        grid_spec=pltpu.PrefetchScalarGridSpec(
            num_scalar_prefetch=2,
            grid=(4,),
            in_specs=[whole] * 8,
            out_specs=pl.BlockSpec((1, 8, 2, *part[1:]), lambda b, *_: (b, 0, 0, 0, 0)),
        ),
        out_shape=jax.ShapeDtypeStruct((4, 8, 2, *part[1:]), jnp.bfloat16),
        compiler_params=pltpu.CompilerParams(vmem_limit_bytes=32 << 20),
        cost_estimate=pl.CostEstimate(flops=0, bytes_accessed=16 * rows * width, transcendentals=0),
        name="place_blocks",
    )(distance, core, *[v.reshape(part) for v in mine + theirs])
    return out.reshape(4, 2 * rows, width)


def summed(value, axis):
    n = SIZES[axis]
    apart = 1
    while apart < n:
        value = value + lax.ppermute(value, axis, [(i, i ^ apart) for i in range(n)])
        apart *= 2
    return value


def product_kernel(transposing, order, slot, left, grads, near, far, *turned):
    if transposing:
        lefts = turned[0]
        for i in range(0, left.shape[1], 128):
            lefts[i : i + 128, :] = left[:, i : i + 128].T
    else:
        lefts = left
    cols = near.shape[-1]
    for j in range(4):
        rows = pl.ds(pl.multiple_of(order[j] * 192, 192), 192)
        value = jnp.dot(lefts[rows, :], grads[...], preferred_element_type=jnp.float32)
        out = (near, far)[j // 2]
        for b in range(4):
            out[slot[b], j % 2] = value[:, b * cols : (b + 1) * cols].astype(out.dtype)


def product(order, slot, left, grads, kind, transposing):
    tokens, width = grads.shape
    shape = jax.ShapeDtypeStruct((4, 2, width // 8, width // 4), kind)
    outs = [shape, shape]
    if transposing:
        outs.append(jax.ShapeDtypeStruct((width, tokens), left.dtype))
    smem, vmem = (pl.BlockSpec(memory_space=m) for m in (pltpu.SMEM, pltpu.VMEM))
    return pl.pallas_call(
        lambda *refs: product_kernel(transposing, *refs),
        in_specs=[smem, smem, vmem, vmem],
        out_specs=[vmem] * len(outs),
        out_shape=outs,
        compiler_params=pltpu.CompilerParams(vmem_limit_bytes=40 << 20),
        cost_estimate=pl.CostEstimate(
            flops=tokens * width * width, bytes_accessed=12 << 20, transcendentals=0
        ),
        name="product",
    )(order, slot, left, grads)


def left_kernel(place, left, mine, theirs, adam, out, squares, both):
    rows = both.shape[2]
    for e in range(8):
        at = (place[0] + 8 - e) % 8
        both[at, place[1]] = mine[e, :rows]
        both[at, 1 - place[1]] = theirs[e, :rows]
    right = both[...].reshape(left.shape[1], out.shape[1])
    value = jnp.dot(left[...], right, preferred_element_type=jnp.float32)
    out[...] = value
    row = lax.broadcasted_iota(jnp.int32, squares.shape, 0)
    squares[...] = jnp.where(row == 0, adam[...], jnp.sum(value * value))


def left_product(place, left, mine, theirs, adam):
    width = mine.shape[-1]
    rows = left.shape[1] // 16
    vmem = pl.BlockSpec(memory_space=pltpu.VMEM)
    return pl.pallas_call(
        left_kernel,
        in_specs=[pl.BlockSpec(memory_space=pltpu.SMEM)] + [vmem] * 4,
        out_specs=[vmem] * 2,
        out_shape=[
            jax.ShapeDtypeStruct((left.shape[0], width), jnp.float32),
            jax.ShapeDtypeStruct((8, 128), jnp.float32),
        ],
        scratch_shapes=[pltpu.VMEM((8, 2, rows, width), jnp.bfloat16)],
        compiler_params=pltpu.CompilerParams(vmem_limit_bytes=32 << 20),
        cost_estimate=pl.CostEstimate(
            flops=2 * left.shape[0] * left.shape[1] * width,
            bytes_accessed=6 << 20,
            transcendentals=0,
        ),
        name="left_product",
    )(place, left, mine, theirs, adam)


def root_pairs():
    pairs = []
    for z in range(8):
        for c in range(2):
            for y in range(4):
                line = ((z % 2) * 4 + y) * 2 + c
                pairs.append(((z * 2 + c) * 4 + y, line * 4 + z // 2))
    return pairs


def body(
    activations,
    output_grads,
    owner,
    step_count,
    statistics,
    inverse_roots,
    first_moment,
    second_moment,
):
    bf, f32 = (jnp.bfloat16, jnp.float32)
    width = activations.shape[1]
    blocks, cols = output_grads.shape[1:]
    span = statistics.shape[0]
    slab = 4 * span
    x, z, core, y = (lax.axis_index(a) for a in EVERY)
    right_rows = lax.ppermute(inverse_roots[:, 1, :], PLANE, root_pairs())
    rows = jnp.concatenate([right_rows, inverse_roots[:, 0, :]], 0)
    roots = lax.all_gather(rows, "z", axis=0, tiled=True)

    order = jnp.array([[4, 3, 2, 1], [0, 5, 6, 7]], jnp.int32)
    orders = (z + jnp.where(core == 0, order, order[::-1])) % 8
    slot = (owner - x) % 4
    grads = output_grads.reshape(activations.shape[0], blocks * cols)
    *theirs, turned = product(orders[1], slot, activations, grads, bf, True)
    own = product(orders[0], slot, turned, grads, f32, False)
    theirs[0], _ = lax.optimization_barrier((theirs[0], right_rows))

    chunks = []
    for mine, other in zip(own, theirs):
        pair = mine + shifted(other, "c", 1).astype(f32)
        total = pair[0]
        for d in (2, 1, 3):
            total = total + shifted(pair[d].astype(bf), "x", d).astype(f32)
        chunks.append(total)
    roots, _ = lax.optimization_barrier((roots, chunks))
    roots = roots.reshape(8, 2, span, width)
    right_half = roots[:, 0].reshape(8 * span, width)
    right_other = shifted(right_half, "c", 1)
    left_root = lax.all_gather(roots[:, 1].reshape(8 * span, width), "y", axis=0)
    left_root = left_root.reshape(4, 8, span, width).transpose(1, 0, 2, 3).reshape(8 * slab, width)

    half = jnp.where(core == 1, chunks[0][0], 0.0)
    for k, piece in ((4, chunks[0][0]), (3, chunks[0][1]), (2, chunks[1][0]), (1, chunks[1][1])):
        half = half + both_ways(piece.astype(bf), k).astype(f32)
    half = half.reshape(2, slab, cols)
    reduced = lax.dynamic_index_in_dim(half, core, 0, keepdims=False) + shifted(
        lax.dynamic_index_in_dim(half, 1 - core, 0, keepdims=False), "c", 1
    )
    slab_rows = gathered(reduced.astype(bf), "y", 1)

    right_root = by_core(
        right_half.reshape(2, 4, span, width), right_other.reshape(2, 4, span, width), core, 1
    ).reshape(cols, width)
    right_part = lax.dot_general(
        slab_rows, right_root, (((1,), (1,)), ((), ())), preferred_element_type=f32
    ).astype(bf)

    parts = [right_part] + [None] * 7
    for d in outward(8):
        parts[d] = shifted(right_part, "z", d)
    part_half = jnp.stack(parts)

    rounded = lax.dynamic_slice_in_dim(slab_rows, y * span, span, 0)
    exact = rounded.astype(f32)
    first_new = beta_first * first_moment + (1.0 - beta_first) * exact
    second_new = beta_second * second_moment + (1.0 - beta_second) * exact * exact
    count = step_count[0].astype(f32)
    first_hat = first_new / (1.0 - jnp.power(beta_first, count))
    second_hat = second_new / (1.0 - jnp.power(beta_second, count))
    adam = first_hat / (jnp.sqrt(second_hat) + eps_adam)
    adam_squares = summed(jnp.full((8, 128), jnp.sum(adam * adam)), "z")
    part_half, adam_squares = lax.optimization_barrier((part_half, adam_squares))
    precond, squares = left_product(
        jnp.stack([z, core]), left_root, part_half, shifted(part_half, "c", 1), adam_squares
    )
    squares = summed(summed(squares, "c"), "y")
    scale = jnp.sqrt(squares[0, 0]) / (jnp.sqrt(squares[1, 0]) + eps_norm)
    grafted = (precond * scale).astype(bf)
    mine, theirs = ([grafted] * 4, [shifted(grafted, "c", 1)] * 4)
    for d in (2, 1, 3):
        mine[d] = shifted(grafted, "x", d)

    behind, _ = lax.optimization_barrier((slab_rows, part_half))
    half_grad = lax.all_gather(behind, "z", axis=0, tiled=True)
    half_grad, _ = lax.optimization_barrier((half_grad, mine[1]))
    pair_rows = jnp.concatenate([rounded, shifted(rounded, "c", 1)], 0)
    left_grams = lax.dot_general(
        pair_rows, half_grad, (((1,), (1,)), ((), ())), preferred_element_type=f32
    )
    base = z * 2 * slab + y * span
    pair_columns = jnp.concatenate(
        [
            lax.dynamic_slice_in_dim(half_grad, base + k * slab, span, 1)
            for k in (core, 1 - core)
        ],
        1,
    )
    right_grams = lax.dot_general(
        pair_columns, half_grad, (((0,), (0,)), ((), ())), preferred_element_type=f32
    )
    left_gram = by_core(
        left_grams[:span].reshape(span, 8, slab),
        shifted(left_grams[span:], "c", 1).reshape(span, 8, slab),
        core,
        2,
    ).reshape(span, width)
    right_gram = right_grams[:span] + shifted(right_grams[span:], "c", 1)
    new_stats = beta_stat * statistics + (1.0 - beta_stat) * jnp.stack([left_gram, right_gram], 1)
    for d in (1, 3, 2):
        theirs[d] = shifted(mine[d], "c", 1)
    theirs[2], new_stats = lax.optimization_barrier((theirs[2], new_stats))
    update = place_blocks((x - owner) % 4, core.reshape(1), mine, theirs)
    return (new_stats, first_new, second_new, update)


def solution(mesh):
    torus = Mesh(mesh.devices.reshape(*SIZES.values()), EVERY)
    placed = (
        P(REPLICA, None),
        P(REPLICA, None, "y"),
        P(),
        P(),
        P(EVERY, None, None),
        P(EVERY, None, None),
        P(EVERY, None),
        P(EVERY, None),
    )
    return jax.shard_map(
        body,
        mesh=torus,
        in_specs=placed,
        out_specs=(P(EVERY, None, None), P(EVERY, None), P(EVERY, None), P(None, None, "y")),
        check_vma=False,
    )
```

```python
import jax
import jax.numpy as jnp
from jax import lax
from jax.experimental import pallas as pl
from jax.experimental.pallas import tpu as pltpu
from jax.sharding import Mesh
from jax.sharding import PartitionSpec as P

SIZES = {"x": 4, "z": 8, "c": 2, "y": 4}
REPLICA = ("x", "z", "c")
EVERY = ("x", "z", "c", "y")
PLANE = ("z", "c", "y")

beta_stat = 0.9
beta_first = 0.9
beta_second = 0.999
eps_adam = 1e-08
eps_norm = 1e-06


def shifted(value, axis, by):
    n = SIZES[axis]
    return lax.ppermute(value, axis, [(i, (i + by) % n) for i in range(n)])


def outward(n):
    return sorted(range(1, n), key=lambda d: -min(d, n - d))


def both_ways(value, apart):
    pairs = [(2 * i, 2 * ((i + apart) % 8)) for i in range(8)]
    if apart != 4:
        pairs += [(2 * i + 1, 2 * ((i - apart) % 8) + 1) for i in range(8)]
    return lax.ppermute(value, ("z", "c"), pairs)


def by_core(mine, theirs, core, dim):
    return jnp.where(
        core == 0, jnp.stack([mine, theirs], dim), jnp.stack([theirs, mine], dim)
    )


def place_kernel(distance, core, *refs):
    out = refs[-1]
    mine, theirs = (refs[:4], refs[4:8])
    block = pl.program_id(0)
    for d in range(4):
        for k in range(2):

            @pl.when((distance[block] == d) & (core[0] == k))
            def _():
                out[0, :, k] = mine[d][...]
                out[0, :, 1 - k] = theirs[d][...]


def place_blocks(distance, core, mine, theirs):
    rows, width = mine[0].shape
    part = (8, rows // 8, width)
    whole = pl.BlockSpec(part, lambda b, *_: (0, 0, 0))
    out = pl.pallas_call(
        place_kernel,
        grid_spec=pltpu.PrefetchScalarGridSpec(
            num_scalar_prefetch=2,
            grid=(4,),
            in_specs=[whole] * 8,
            out_specs=pl.BlockSpec((1, 8, 2, *part[1:]), lambda b, *_: (b, 0, 0, 0, 0)),
        ),
        out_shape=jax.ShapeDtypeStruct((4, 8, 2, *part[1:]), jnp.bfloat16),
        compiler_params=pltpu.CompilerParams(vmem_limit_bytes=32 << 20),
        cost_estimate=pl.CostEstimate(flops=0, bytes_accessed=16 * rows * width, transcendentals=0),
        name="place_blocks",
    )(distance, core, *[v.reshape(part) for v in mine + theirs])
    return out.reshape(4, 2 * rows, width)


def total_of(first, others):
    for value in others:
        first = first + value.astype(jnp.float32)
    return first


def product_kernel(transposing, order, slot, left, grads, near, far, *turned):
    if transposing:
        lefts = turned[0]
        for i in range(0, left.shape[1], 128):
            lefts[i : i + 128, :] = left[:, i : i + 128].T
    else:
        lefts = left
    cols = near.shape[-1]
    for j in range(4):
        rows = pl.ds(pl.multiple_of(order[j] * 192, 192), 192)
        value = jnp.dot(lefts[rows, :], grads[...], preferred_element_type=jnp.float32)
        out = (near, far)[j // 2]
        for b in range(4):
            out[slot[b], j % 2] = value[:, b * cols : (b + 1) * cols].astype(out.dtype)


def product(order, slot, left, grads, kind, transposing):
    tokens, width = grads.shape
    shape = jax.ShapeDtypeStruct((4, 2, width // 8, width // 4), kind)
    outs = [shape, shape]
    if transposing:
        outs.append(jax.ShapeDtypeStruct((width, tokens), left.dtype))
    smem, vmem = (pl.BlockSpec(memory_space=m) for m in (pltpu.SMEM, pltpu.VMEM))
    return pl.pallas_call(
        lambda *refs: product_kernel(transposing, *refs),
        in_specs=[smem, smem, vmem, vmem],
        out_specs=[vmem] * len(outs),
        out_shape=outs,
        compiler_params=pltpu.CompilerParams(vmem_limit_bytes=40 << 20),
        cost_estimate=pl.CostEstimate(
            flops=tokens * width * width, bytes_accessed=12 << 20, transcendentals=0
        ),
        name="product",
    )(order, slot, left, grads)


def right_kernel(line, bias, root, first, second, *refs):
    pieces, (part, rows, rounded, new_first, new_second) = (refs[:4], refs[4:])
    slab, cols = pieces[0].shape
    span = first.shape[0]
    total = jnp.zeros((slab, cols), jnp.float32)
    for d in range(4):
        at = pl.ds(pl.multiple_of((line[0] + 4 - d) % 4 * cols, 128), cols)
        rows[:, at] = pieces[d][...]
        total += lax.dot_general(
            pieces[d][...],
            root[:, at],
            (((1,), (1,)), ((), ())),
            preferred_element_type=jnp.float32,
        )
    part[:slab] = total.astype(part.dtype)

    at = (32, slab)
    wanted = lax.broadcasted_iota(jnp.int32, at, 0) + line[0] * span
    pick = jnp.where(lax.broadcasted_iota(jnp.int32, at, 1) == wanted, 1.0, 0.0)
    exact = jnp.dot(
        pick.astype(jnp.bfloat16), rows[...], preferred_element_type=jnp.float32
    )[:span]
    rounded[...] = exact.astype(rounded.dtype)
    first_new = beta_first * first[...] + (1.0 - beta_first) * exact
    second_new = beta_second * second[...] + (1.0 - beta_second) * exact * exact
    new_first[...] = first_new
    new_second[...] = second_new
    adam = (first_new / bias[0]) / (jnp.sqrt(second_new / bias[1]) + eps_adam)
    value = jnp.full((16, cols), jnp.sum(adam * adam), jnp.float32)
    row = lax.broadcasted_iota(jnp.int32, value.shape, 0)
    ride = jnp.zeros(value.shape, jnp.float32)
    for k in range(3):
        top = value.astype(jnp.bfloat16).astype(jnp.float32)
        ride = jnp.where(row == k, top, ride)
        value = value - top
    part[slab:] = ride.astype(part.dtype)


def right_product(line, bias, root, first, second, pieces):
    slab, cols = pieces[0].shape
    smem, vmem = (pl.BlockSpec(memory_space=m) for m in (pltpu.SMEM, pltpu.VMEM))
    bf = jnp.bfloat16
    return pl.pallas_call(
        right_kernel,
        in_specs=[smem] * 2 + [vmem] * 7,
        out_specs=[vmem] * 5,
        out_shape=[
            jax.ShapeDtypeStruct((slab + 16, cols), bf),
            jax.ShapeDtypeStruct((slab, 4 * cols), bf),
            jax.ShapeDtypeStruct(first.shape, bf),
            jax.ShapeDtypeStruct(first.shape, first.dtype),
            jax.ShapeDtypeStruct(second.shape, second.dtype),
        ],
        compiler_params=pltpu.CompilerParams(vmem_limit_bytes=16 << 20),
        cost_estimate=pl.CostEstimate(
            flops=8 * slab * cols * cols, bytes_accessed=2 << 20, transcendentals=0
        ),
        name="right_product",
    )(line, bias, root, first, second, *pieces)


def left_kernel(place, own, mine, theirs, *refs):
    lefts, out, squares, both = refs
    z, core = (place[0], place[1])
    slab = both.shape[2]
    both[z] = own[:, :slab]
    for k in (1, 2, 3):
        up, down = ((z + k) % 8, (z + 8 - k) % 8)
        two = slice(2 * k - 2, 2 * k)
        both[jnp.where(core == 0, down, up)] = mine[two, :slab]
        both[jnp.where(core == 0, up, down)] = theirs[two, :slab]
    both[(z + 4) % 8, core] = mine[6, :slab]
    both[(z + 4) % 8, 1 - core] = theirs[6, :slab]
    adam = jnp.zeros((16, 128), jnp.float32)
    for ref in (own, mine, theirs):
        for k in range(ref.shape[0]):
            adam += ref[k, slab:, :128].astype(jnp.float32)
    width = out.shape[-1]
    right = both[...].reshape(16 * slab, width)
    total = jnp.zeros((), jnp.float32)
    for d in range(4):
        value = jnp.dot(lefts[d], right, preferred_element_type=jnp.float32)
        total += jnp.sum(value * value)
        span = value.shape[0] // 8
        for k in range(8):
            out[k, d * span : (d + 1) * span] = value[k * span : (k + 1) * span]
    column = lax.broadcasted_iota(jnp.int32, adam.shape, 1)
    adam = 0.5 * jnp.sum(jnp.where(column == 0, adam, 0.0))
    row = lax.broadcasted_iota(jnp.int32, squares.shape, 0)
    squares[...] = jnp.where(row == 0, adam, total)


def left_product(place, lefts, own, mine, theirs):
    _, rows, width = lefts.shape
    slab, cols = (width // 16, own.shape[-1])
    smem, vmem = (pl.BlockSpec(memory_space=m) for m in (pltpu.SMEM, pltpu.VMEM))
    out, squares = pl.pallas_call(
        left_kernel,
        in_specs=[smem] + [vmem] * 4,
        out_specs=[vmem] * 2,
        out_shape=[
            jax.ShapeDtypeStruct((8, slab, cols), jnp.float32),
            jax.ShapeDtypeStruct((8, 128), jnp.float32),
        ],
        scratch_shapes=[pltpu.VMEM((8, 2, slab, cols), jnp.bfloat16)],
        compiler_params=pltpu.CompilerParams(vmem_limit_bytes=32 << 20),
        cost_estimate=pl.CostEstimate(
            flops=8 * rows * width * cols, bytes_accessed=6 << 20, transcendentals=0
        ),
        name="left_product",
    )(place, own, mine, theirs, lefts)
    return out.reshape(8 * slab, cols), squares


def grams_kernel(first, rows, grad, kept, sent):
    span = rows.shape[0] // 2
    slab, width = grad.shape
    across = (((1,), (1,)), ((), ()))
    left = lax.dot_general(rows[...], grad[...], across, preferred_element_type=jnp.float32)
    at = (2 * span, width)
    row = lax.broadcasted_iota(jnp.int32, at, 0)
    wanted = jnp.where(row < span, row + first[0], row + first[1] - span)
    pick = jnp.where(lax.broadcasted_iota(jnp.int32, at, 1) == wanted, 1.0, 0.0)
    columns = lax.dot_general(
        pick.astype(jnp.bfloat16), grad[...], across, preferred_element_type=jnp.float32
    ).astype(jnp.bfloat16)
    right = jnp.dot(columns, grad[...], preferred_element_type=jnp.float32)
    for out, which in ((kept, slice(0, span)), (sent, slice(span, 2 * span))):
        out[:, :slab] = left[which]
        out[:, slab:] = right[which]


def grams(first, rows, grad):
    span = rows.shape[0] // 2
    slab, width = grad.shape
    smem, vmem = (pl.BlockSpec(memory_space=m) for m in (pltpu.SMEM, pltpu.VMEM))
    return pl.pallas_call(
        grams_kernel,
        in_specs=[smem] + [vmem] * 2,
        out_specs=[vmem] * 2,
        out_shape=[jax.ShapeDtypeStruct((span, slab + width), jnp.float32)] * 2,
        compiler_params=pltpu.CompilerParams(vmem_limit_bytes=24 << 20),
        cost_estimate=pl.CostEstimate(
            flops=12 * span * slab * width, bytes_accessed=3 << 20, transcendentals=0
        ),
        name="grams",
    )(first, rows, grad)


def stats_kernel(core, mine, theirs, old, new):
    width = old.shape[-1]
    slab = width // 16
    for k in range(2):

        @pl.when(core[0] == k)
        def _():
            for half, part in ((k, mine), (1 - k, theirs)):
                for z in range(8):
                    at = slice((2 * z + half) * slab, (2 * z + half + 1) * slab)
                    new[:, 0, at] = (
                        beta_stat * old[:, 0, at]
                        + (1.0 - beta_stat) * part[:, z * slab : (z + 1) * slab]
                    )

    right = mine[:, width // 2 :] + theirs[:, width // 2 :]
    new[:, 1, :] = beta_stat * old[:, 1, :] + (1.0 - beta_stat) * right


def new_statistics(core, mine, theirs, old):
    smem, vmem = (pl.BlockSpec(memory_space=m) for m in (pltpu.SMEM, pltpu.VMEM))
    return pl.pallas_call(
        stats_kernel,
        in_specs=[smem] + [vmem] * 3,
        out_specs=vmem,
        out_shape=jax.ShapeDtypeStruct(old.shape, old.dtype),
        compiler_params=pltpu.CompilerParams(vmem_limit_bytes=16 << 20),
        cost_estimate=pl.CostEstimate(flops=0, bytes_accessed=1 << 20, transcendentals=0),
        name="new_statistics",
    )(core, mine, theirs, old)


def root_pairs():
    pairs = []
    for z in range(8):
        for c in range(2):
            for y in range(4):
                line = ((z % 2) * 4 + y) * 2 + c
                pairs.append(((z * 2 + c) * 4 + y, line * 4 + z // 2))
    return pairs


def body(
    activations,
    output_grads,
    owner,
    step_count,
    statistics,
    inverse_roots,
    first_moment,
    second_moment,
):
    bf, f32 = (jnp.bfloat16, jnp.float32)
    width = activations.shape[1]
    blocks, cols = output_grads.shape[1:]
    span = statistics.shape[0]
    slab = 4 * span
    x, z, core, y = (lax.axis_index(a) for a in EVERY)
    right_rows = lax.ppermute(inverse_roots[:, 1, :], PLANE, root_pairs())
    order = jnp.array([[4, 3, 2, 1], [0, 5, 6, 7]], jnp.int32)
    orders = (z + jnp.where(core == 0, order, order[::-1])) % 8
    slot = (owner - x) % 4
    grads = output_grads.reshape(activations.shape[0], blocks * cols)
    *theirs, turned = product(orders[1], slot, activations, grads, bf, True)
    rows = jnp.concatenate([right_rows, inverse_roots[:, 0, :]], 0)
    roots = lax.all_gather(rows, "z", axis=0, tiled=True)
    own = product(orders[0], slot, turned, grads, f32, False)

    pairs = [mine + shifted(other, "c", 1).astype(f32) for mine, other in zip(own, theirs)]
    came = [[shifted(pair[d].astype(bf), "x", d) for d in (2, 1, 3)] for pair in pairs]
    near = total_of(pairs[0][0], came[0])
    half = jnp.where(core == 1, near[0], 0.0)
    came_z = [both_ways(near[0].astype(bf), 4), both_ways(near[1].astype(bf), 3)]
    came[1], came_z = lax.optimization_barrier((came[1], came_z))
    far = total_of(pairs[1][0], came[1])
    came_z += [both_ways(far[0].astype(bf), 2), both_ways(far[1].astype(bf), 1)]
    came_z, roots = lax.optimization_barrier((came_z, roots))
    half = total_of(half, came_z)

    roots = roots.reshape(8, 2, span, width)
    right_half = roots[:, 0].reshape(8 * span, width)
    right_other = shifted(right_half, "c", 1)
    lefts = lax.all_gather(roots[:, 1].reshape(8 * span, width), "y", axis=0)

    half = half.reshape(2, slab, cols)
    reduced = lax.dynamic_index_in_dim(half, core, 0, keepdims=False) + shifted(
        lax.dynamic_index_in_dim(half, 1 - core, 0, keepdims=False), "c", 1
    )
    slab_grad = reduced.astype(bf)
    pieces = [slab_grad] + [shifted(slab_grad, "y", d) for d in (2, 1, 3)]
    pieces = [pieces[0], pieces[2], pieces[1], pieces[3]]

    right_root = by_core(
        right_half.reshape(2, 4, span, width), right_other.reshape(2, 4, span, width), core, 1
    ).reshape(cols, width)
    count = step_count[0].astype(f32)
    bias = jnp.stack([1.0 - jnp.power(beta_first, count), 1.0 - jnp.power(beta_second, count)])
    part, slab_rows, rounded, first_new, second_new = right_product(
        y.reshape(1), bias, right_root, first_moment, second_moment, pieces
    )
    pair_part = by_core(part, shifted(part, "c", 1), core, 0)
    parts = [both_ways(pair_part, k) for k in (1, 2, 3)] + [shifted(part[None], "z", 4)]
    parts, lefts, slab_rows = lax.optimization_barrier((jnp.concatenate(parts), lefts, slab_rows))
    precond, squares = left_product(
        jnp.stack([z, core]), lefts, pair_part, parts, shifted(parts, "c", 1)
    )
    squares = squares + shifted(squares, "c", 1)
    squares = squares + sum(shifted(squares, "y", d) for d in (2, 1, 3))
    scale = jnp.sqrt(squares[0, 0]) / (jnp.sqrt(squares[1, 0]) + eps_norm)
    grafted = (precond * scale).astype(bf)
    mine, theirs = ([grafted] * 4, [shifted(grafted, "c", 1)] * 4)
    for d in (2, 1, 3):
        mine[d] = shifted(grafted, "x", d)

    half_grad = lax.all_gather(slab_rows, "z", axis=0, tiled=True)
    pair_rows = jnp.concatenate([rounded, shifted(rounded, "c", 1)], 0)
    half_grad, mine[1], mine[3] = lax.optimization_barrier((half_grad, mine[1], mine[3]))
    base = z * 2 * slab + y * span
    kept, sent = grams(
        jnp.stack([base + core * slab, base + (1 - core) * slab]), pair_rows, half_grad
    )
    mine, sent = lax.optimization_barrier((mine, sent))
    for d in (1, 2, 3):
        theirs[d] = shifted(mine[d], "c", 1)
    new_stats = new_statistics(core.reshape(1), kept, shifted(sent, "c", 1), statistics)
    update = place_blocks((x - owner) % 4, core.reshape(1), mine, theirs)
    return (new_stats, first_new, second_new, update)


def solution(mesh):
    torus = Mesh(mesh.devices.reshape(*SIZES.values()), EVERY)
    placed = (
        P(REPLICA, None),
        P(REPLICA, None, "y"),
        P(),
        P(),
        P(EVERY, None, None),
        P(EVERY, None, None),
        P(EVERY, None),
        P(EVERY, None),
    )
    return jax.shard_map(
        body,
        mesh=torus,
        in_specs=placed,
        out_specs=(P(EVERY, None, None), P(EVERY, None), P(EVERY, None), P(None, None, "y")),
        check_vma=False,
    )
```

```python
import jax
import jax.numpy as jnp
from jax import lax
from jax.experimental import pallas as pl
from jax.experimental.pallas import tpu as pltpu
from jax.sharding import Mesh
from jax.sharding import PartitionSpec as P

SIZES = {"x": 4, "z": 8, "c": 2, "y": 4}
REPLICA = ("x", "z", "c")
EVERY = ("x", "z", "c", "y")

beta_stat = 0.9
beta_first = 0.9
beta_second = 0.999
eps_adam = 1e-08
eps_norm = 1e-06


def shifted(value, axis, by):
    n = SIZES[axis]
    return lax.ppermute(value, axis, [(i, (i + by) % n) for i in range(n)])


def outward(n):
    return sorted(range(1, n), key=lambda d: -min(d, n - d))


def both_ways(value, apart):
    pairs = [(2 * i, 2 * ((i + apart) % 8)) for i in range(8)]
    if apart != 4:
        pairs += [(2 * i + 1, 2 * ((i - apart) % 8) + 1) for i in range(8)]
    return lax.ppermute(value, ("z", "c"), pairs)


def by_core(mine, theirs, core, dim):
    return jnp.where(
        core == 0, jnp.stack([mine, theirs], dim), jnp.stack([theirs, mine], dim)
    )


def place_kernel(distance, core, *refs):
    out = refs[-1]
    mine, theirs = (refs[:4], refs[4:8])
    block = pl.program_id(0)
    for d in range(4):
        for k in range(2):

            @pl.when((distance[block] == d) & (core[0] == k))
            def _():
                out[0, :, k] = mine[d][...]
                out[0, :, 1 - k] = theirs[d][...]


def place_blocks(distance, core, mine, theirs):
    rows, width = mine[0].shape
    part = (8, rows // 8, width)
    whole = pl.BlockSpec(part, lambda b, *_: (0, 0, 0))
    out = pl.pallas_call(
        place_kernel,
        grid_spec=pltpu.PrefetchScalarGridSpec(
            num_scalar_prefetch=2,
            grid=(4,),
            in_specs=[whole] * 8,
            out_specs=pl.BlockSpec((1, 8, 2, *part[1:]), lambda b, *_: (b, 0, 0, 0, 0)),
        ),
        out_shape=jax.ShapeDtypeStruct((4, 8, 2, *part[1:]), jnp.bfloat16),
        compiler_params=pltpu.CompilerParams(vmem_limit_bytes=32 << 20),
        cost_estimate=pl.CostEstimate(flops=0, bytes_accessed=16 * rows * width, transcendentals=0),
        name="place_blocks",
    )(distance, core, *[v.reshape(part) for v in mine + theirs])
    return out.reshape(4, 2 * rows, width)


def total_of(first, others):
    for value in others:
        first = first + value.astype(jnp.float32)
    return first


def product_kernel(transposing, order, slot, left, grads, near, far, *turned):
    if transposing:
        lefts = turned[0]
        for i in range(0, left.shape[1], 128):
            lefts[i : i + 128, :] = left[:, i : i + 128].T
    else:
        lefts = left
    cols = near.shape[-1]
    for j in range(4):
        rows = pl.ds(pl.multiple_of(order[j] * 192, 192), 192)
        value = jnp.dot(lefts[rows, :], grads[...], preferred_element_type=jnp.float32)
        out = (near, far)[j // 2]
        for b in range(4):
            out[slot[b], j % 2] = value[:, b * cols : (b + 1) * cols].astype(out.dtype)


def product(order, slot, left, grads, kind, transposing):
    tokens, width = grads.shape
    shape = jax.ShapeDtypeStruct((4, 2, width // 8, width // 4), kind)
    outs = [shape, shape]
    if transposing:
        outs.append(jax.ShapeDtypeStruct((width, tokens), left.dtype))
    smem, vmem = (pl.BlockSpec(memory_space=m) for m in (pltpu.SMEM, pltpu.VMEM))
    return pl.pallas_call(
        lambda *refs: product_kernel(transposing, *refs),
        in_specs=[smem, smem, vmem, vmem],
        out_specs=[vmem] * len(outs),
        out_shape=outs,
        compiler_params=pltpu.CompilerParams(vmem_limit_bytes=40 << 20),
        cost_estimate=pl.CostEstimate(
            flops=tokens * width * width, bytes_accessed=12 << 20, transcendentals=0
        ),
        name="product",
    )(order, slot, left, grads)


def right_kernel(line, bias, root, first, second, *refs):
    pieces, (part, rows, rounded, new_first, new_second) = (refs[:4], refs[4:])
    slab, cols = pieces[0].shape
    span = first.shape[0]
    total = jnp.zeros((slab, cols), jnp.float32)
    for d in range(4):
        at = pl.ds(pl.multiple_of((line[0] + 4 - d) % 4 * cols, 128), cols)
        rows[:, at] = pieces[d][...]
        total += lax.dot_general(
            pieces[d][...],
            root[:, at],
            (((1,), (1,)), ((), ())),
            preferred_element_type=jnp.float32,
        )
    part[:slab] = total.astype(part.dtype)

    at = (32, slab)
    wanted = lax.broadcasted_iota(jnp.int32, at, 0) + line[0] * span
    pick = jnp.where(lax.broadcasted_iota(jnp.int32, at, 1) == wanted, 1.0, 0.0)
    exact = jnp.dot(
        pick.astype(jnp.bfloat16), rows[...], preferred_element_type=jnp.float32
    )[:span]
    rounded[...] = exact.astype(rounded.dtype)
    first_new = beta_first * first[...] + (1.0 - beta_first) * exact
    second_new = beta_second * second[...] + (1.0 - beta_second) * exact * exact
    new_first[...] = first_new
    new_second[...] = second_new
    adam = (first_new / bias[0]) / (jnp.sqrt(second_new / bias[1]) + eps_adam)
    value = jnp.full((16, cols), jnp.sum(adam * adam), jnp.float32)
    row = lax.broadcasted_iota(jnp.int32, value.shape, 0)
    ride = jnp.zeros(value.shape, jnp.float32)
    for k in range(3):
        top = value.astype(jnp.bfloat16).astype(jnp.float32)
        ride = jnp.where(row == k, top, ride)
        value = value - top
    part[slab:] = ride.astype(part.dtype)


def right_product(line, bias, root, first, second, pieces):
    slab, cols = pieces[0].shape
    smem, vmem = (pl.BlockSpec(memory_space=m) for m in (pltpu.SMEM, pltpu.VMEM))
    bf = jnp.bfloat16
    return pl.pallas_call(
        right_kernel,
        in_specs=[smem] * 2 + [vmem] * 7,
        out_specs=[vmem] * 5,
        out_shape=[
            jax.ShapeDtypeStruct((slab + 16, cols), bf),
            jax.ShapeDtypeStruct((slab, 4 * cols), bf),
            jax.ShapeDtypeStruct(first.shape, bf),
            jax.ShapeDtypeStruct(first.shape, first.dtype),
            jax.ShapeDtypeStruct(second.shape, second.dtype),
        ],
        compiler_params=pltpu.CompilerParams(vmem_limit_bytes=16 << 20),
        cost_estimate=pl.CostEstimate(
            flops=8 * slab * cols * cols, bytes_accessed=2 << 20, transcendentals=0
        ),
        name="right_product",
    )(line, bias, root, first, second, *pieces)


def left_kernel(place, own, mine, theirs, *refs):
    lefts, out, squares, both = refs
    z, core = (place[0], place[1])
    slab = both.shape[2]
    both[z] = own[:, :slab]
    for k in (1, 2, 3):
        up, down = ((z + k) % 8, (z + 8 - k) % 8)
        two = slice(2 * k - 2, 2 * k)
        both[jnp.where(core == 0, down, up)] = mine[two, :slab]
        both[jnp.where(core == 0, up, down)] = theirs[two, :slab]
    both[(z + 4) % 8, core] = mine[6, :slab]
    both[(z + 4) % 8, 1 - core] = theirs[6, :slab]
    adam = jnp.zeros((16, 128), jnp.float32)
    for ref in (own, mine, theirs):
        for k in range(ref.shape[0]):
            adam += ref[k, slab:, :128].astype(jnp.float32)
    width = out.shape[-1]
    right = both[...].reshape(16 * slab, width)
    total = jnp.zeros((), jnp.float32)
    for d in range(4):
        value = jnp.dot(lefts[d], right, preferred_element_type=jnp.float32)
        total += jnp.sum(value * value)
        span = value.shape[0] // 8
        for k in range(8):
            out[k, d * span : (d + 1) * span] = value[k * span : (k + 1) * span]
    column = lax.broadcasted_iota(jnp.int32, adam.shape, 1)
    adam = 0.5 * jnp.sum(jnp.where(column == 0, adam, 0.0))
    row = lax.broadcasted_iota(jnp.int32, squares.shape, 0)
    squares[...] = jnp.where(row == 0, adam, total)


def left_product(place, lefts, own, mine, theirs):
    _, rows, width = lefts.shape
    slab, cols = (width // 16, own.shape[-1])
    smem, vmem = (pl.BlockSpec(memory_space=m) for m in (pltpu.SMEM, pltpu.VMEM))
    out, squares = pl.pallas_call(
        left_kernel,
        in_specs=[smem] + [vmem] * 4,
        out_specs=[vmem] * 2,
        out_shape=[
            jax.ShapeDtypeStruct((8, slab, cols), jnp.float32),
            jax.ShapeDtypeStruct((8, 128), jnp.float32),
        ],
        scratch_shapes=[pltpu.VMEM((8, 2, slab, cols), jnp.bfloat16)],
        compiler_params=pltpu.CompilerParams(vmem_limit_bytes=32 << 20),
        cost_estimate=pl.CostEstimate(
            flops=8 * rows * width * cols, bytes_accessed=6 << 20, transcendentals=0
        ),
        name="left_product",
    )(place, own, mine, theirs, lefts)
    return out.reshape(8 * slab, cols), squares


def grams_kernel(first, rows, grad, kept, sent):
    span = rows.shape[0] // 2
    slab, width = grad.shape
    across = (((1,), (1,)), ((), ()))
    left = lax.dot_general(rows[...], grad[...], across, preferred_element_type=jnp.float32)
    at = (2 * span, width)
    row = lax.broadcasted_iota(jnp.int32, at, 0)
    wanted = jnp.where(row < span, row + first[0], row + first[1] - span)
    pick = jnp.where(lax.broadcasted_iota(jnp.int32, at, 1) == wanted, 1.0, 0.0)
    columns = lax.dot_general(
        pick.astype(jnp.bfloat16), grad[...], across, preferred_element_type=jnp.float32
    ).astype(jnp.bfloat16)
    right = jnp.dot(columns, grad[...], preferred_element_type=jnp.float32)
    for out, which in ((kept, slice(0, span)), (sent, slice(span, 2 * span))):
        out[:, :slab] = left[which]
        out[:, slab:] = right[which]


def grams(first, rows, grad):
    span = rows.shape[0] // 2
    slab, width = grad.shape
    smem, vmem = (pl.BlockSpec(memory_space=m) for m in (pltpu.SMEM, pltpu.VMEM))
    return pl.pallas_call(
        grams_kernel,
        in_specs=[smem] + [vmem] * 2,
        out_specs=[vmem] * 2,
        out_shape=[jax.ShapeDtypeStruct((span, slab + width), jnp.float32)] * 2,
        compiler_params=pltpu.CompilerParams(vmem_limit_bytes=24 << 20),
        cost_estimate=pl.CostEstimate(
            flops=12 * span * slab * width, bytes_accessed=3 << 20, transcendentals=0
        ),
        name="grams",
    )(first, rows, grad)


def stats_kernel(core, mine, theirs, old, new):
    width = old.shape[-1]
    slab = width // 16
    for k in range(2):

        @pl.when(core[0] == k)
        def _():
            for half, part in ((k, mine), (1 - k, theirs)):
                for z in range(8):
                    at = slice((2 * z + half) * slab, (2 * z + half + 1) * slab)
                    new[:, 0, at] = (
                        beta_stat * old[:, 0, at]
                        + (1.0 - beta_stat) * part[:, z * slab : (z + 1) * slab]
                    )

    right = mine[:, width // 2 :] + theirs[:, width // 2 :]
    new[:, 1, :] = beta_stat * old[:, 1, :] + (1.0 - beta_stat) * right


def new_statistics(core, mine, theirs, old):
    smem, vmem = (pl.BlockSpec(memory_space=m) for m in (pltpu.SMEM, pltpu.VMEM))
    return pl.pallas_call(
        stats_kernel,
        in_specs=[smem] + [vmem] * 3,
        out_specs=vmem,
        out_shape=jax.ShapeDtypeStruct(old.shape, old.dtype),
        compiler_params=pltpu.CompilerParams(vmem_limit_bytes=16 << 20),
        cost_estimate=pl.CostEstimate(flops=0, bytes_accessed=1 << 20, transcendentals=0),
        name="new_statistics",
    )(core, mine, theirs, old)


def body(
    activations,
    output_grads,
    owner,
    step_count,
    statistics,
    inverse_roots,
    first_moment,
    second_moment,
):
    bf, f32 = (jnp.bfloat16, jnp.float32)
    width = activations.shape[1]
    blocks, cols = output_grads.shape[1:]
    span = statistics.shape[0]
    slab = 4 * span
    x, z, core, y = (lax.axis_index(a) for a in EVERY)
    rows = jnp.concatenate([inverse_roots[:, 1, :], inverse_roots[:, 0, :]], 0)
    roots = lax.all_gather(rows, "z", axis=0, tiled=True)

    order = jnp.array([[4, 3, 2, 1], [0, 5, 6, 7]], jnp.int32)
    orders = (z + jnp.where(core == 0, order, order[::-1])) % 8
    slot = (owner - x) % 4
    grads = output_grads.reshape(activations.shape[0], blocks * cols)
    *theirs, turned = product(orders[1], slot, activations, grads, bf, True)
    own = product(orders[0], slot, turned, grads, f32, False)

    pairs = [mine + shifted(other, "c", 1).astype(f32) for mine, other in zip(own, theirs)]
    came = [[shifted(pair[d].astype(bf), "x", d) for d in (2, 1, 3)] for pair in pairs]
    near = total_of(pairs[0][0], came[0])
    half = jnp.where(core == 1, near[0], 0.0)
    came_z = [both_ways(near[0].astype(bf), 4), both_ways(near[1].astype(bf), 3)]
    came[1], came_z, roots = lax.optimization_barrier((came[1], came_z, roots))
    far = total_of(pairs[1][0], came[1])
    came_z += [both_ways(far[0].astype(bf), 2), both_ways(far[1].astype(bf), 1)]
    half = total_of(half, came_z)

    roots = roots.reshape(8, 2, span, width)
    lefts = lax.all_gather(roots[:, 1].reshape(8 * span, width), "y", axis=0)

    wanted = [lax.dynamic_slice_in_dim(roots[:, 0], (y + d) % 4 * 2, 2, 0)[None] for d in range(4)]
    wanted[1:] = [shifted(wanted[d], "y", d) for d in (1, 2, 3)]
    ring = [wanted[(-k) % 4] for k in range(4)]
    right_half = lax.dynamic_slice_in_dim(jnp.concatenate(ring + ring[:-1]), (-y) % 4, 4, 0)
    right_other = shifted(right_half, "c", 1)

    half = half.reshape(2, slab, cols)
    reduced = lax.dynamic_index_in_dim(half, core, 0, keepdims=False) + shifted(
        lax.dynamic_index_in_dim(half, 1 - core, 0, keepdims=False), "c", 1
    )
    slab_grad = reduced.astype(bf)
    pieces = [slab_grad] + [shifted(slab_grad, "y", d) for d in (2, 1, 3)]
    pieces = [pieces[0], pieces[2], pieces[1], pieces[3]]

    right_root = by_core(right_half, right_other, core, 0)
    right_root = right_root.transpose(2, 0, 1, 3, 4).reshape(cols, width)
    count = step_count[0].astype(f32)
    bias = jnp.stack([1.0 - jnp.power(beta_first, count), 1.0 - jnp.power(beta_second, count)])
    part, slab_rows, rounded, first_new, second_new = right_product(
        y.reshape(1), bias, right_root, first_moment, second_moment, pieces
    )
    pair_part = by_core(part, shifted(part, "c", 1), core, 0)
    parts = [both_ways(pair_part, k) for k in (1, 2, 3)] + [shifted(part[None], "z", 4)]
    parts, lefts, slab_rows = lax.optimization_barrier((jnp.concatenate(parts), lefts, slab_rows))
    precond, squares = left_product(
        jnp.stack([z, core]), lefts, pair_part, parts, shifted(parts, "c", 1)
    )
    squares = squares + shifted(squares, "c", 1)
    squares = squares + sum(shifted(squares, "y", d) for d in (2, 1, 3))
    scale = jnp.sqrt(squares[0, 0]) / (jnp.sqrt(squares[1, 0]) + eps_norm)
    grafted = (precond * scale).astype(bf)
    mine, theirs = ([grafted] * 4, [shifted(grafted, "c", 1)] * 4)
    for d in (2, 1, 3):
        mine[d] = shifted(grafted, "x", d)

    half_grad = lax.all_gather(slab_rows, "z", axis=0, tiled=True)
    pair_rows = jnp.concatenate([rounded, shifted(rounded, "c", 1)], 0)
    half_grad, mine[1], mine[3] = lax.optimization_barrier((half_grad, mine[1], mine[3]))
    base = z * 2 * slab + y * span
    kept, sent = grams(
        jnp.stack([base + core * slab, base + (1 - core) * slab]), pair_rows, half_grad
    )
    new_stats = new_statistics(core.reshape(1), kept, shifted(sent, "c", 1), statistics)
    for d in (1, 3):
        theirs[d] = shifted(mine[d], "c", 1)
    mine[2], theirs[1], theirs[3], new_stats = lax.optimization_barrier(
        (mine[2], theirs[1], theirs[3], new_stats)
    )
    theirs[2] = shifted(mine[2], "c", 1)
    update = place_blocks((x - owner) % 4, core.reshape(1), mine, theirs)
    return (new_stats, first_new, second_new, update)


def solution(mesh):
    torus = Mesh(mesh.devices.reshape(*SIZES.values()), EVERY)
    placed = (
        P(REPLICA, None),
        P(REPLICA, None, "y"),
        P(),
        P(),
        P(EVERY, None, None),
        P(EVERY, None, None),
        P(EVERY, None),
        P(EVERY, None),
    )
    return jax.shard_map(
        body,
        mesh=torus,
        in_specs=placed,
        out_specs=(P(EVERY, None, None), P(EVERY, None), P(EVERY, None), P(None, None, "y")),
        check_vma=False,
    )
```
